128 devices in a mesh: req: 32 (over z, y, core), tok: 4 (over x).
Axes of the slice: x: 4, y: 4, z: 4, core: 2. Of those that a mesh axis runs over, the one named last changes fastest.
Arguments:
- tokens: bfloat16 [32768, 2048], P(('req', 'tok')), may hold values from -12 to 12
- attention_norm_gain: float32 [2048], replicated, may hold values from 0.1 to 1.9
- attention_norm_bias: float32 [2048], replicated, may hold values from -1.75 to 1.75
- query_key_value_matrix: bfloat16 [3, 2048, 2048], P(None, 'req', 'tok'), may hold values from -0.125 to 0.125
- query_key_value_bias: float32 [3, 2048], P(None, 'tok'), may hold values from -3 to 3
- output_matrix: bfloat16 [4, 512, 2048], P('tok', 'req'), may hold values from -0.125 to 0.125
- feedforward_norm_gain: float32 [2048], replicated, may hold values from 0.1 to 1.9
- feedforward_norm_bias: float32 [2048], replicated, may hold values from -1.75 to 1.75
- gate_up_matrix: bfloat16 [2, 2048, 2816], P(None, 'req', 'tok'), may hold values from -0.125 to 0.125
- down_matrix: bfloat16 [4, 704, 2048], P('tok', 'req'), may hold values from -0.109375 to 0.109375
- adapter_input_query_key_value: bfloat16 [64, 48, 2048], P(None, None, 'req'), may hold values from -0.125 to 0.125
- adapter_output_query_key_value: bfloat16 [64, 48, 4, 512], P(None, None, 'tok', 'req'), may hold values from -0.75 to 0.75
- adapter_input_output: bfloat16 [64, 16, 4, 512], P(None, None, 'tok', 'req'), may hold values from -0.125 to 0.125
- adapter_output_projection: bfloat16 [64, 16, 2048], P(None, None, 'req'), may hold values from -0.75 to 0.75
- adapter_input_gate_up: bfloat16 [64, 32, 2048], P(None, None, 'req'), may hold values from -0.125 to 0.125
- adapter_output_gate_up: bfloat16 [64, 32, 4, 704], P(None, None, 'tok', 'req'), may hold values from -0.75 to 0.75
- adapter_input_down: bfloat16 [64, 16, 4, 704], P(None, None, 'tok', 'req'), may hold values from -0.109375 to 0.109375
- adapter_output_down: bfloat16 [64, 16, 2048], P(None, None, 'req'), may hold values from -0.75 to 0.75
- lengths: int32 [32, 4], P('req'), may hold values from 1 to 511, 1024 in all within a row
- adapter_per_request: int32 [32, 4], replicated, may hold values from 0 to 63
Outputs:
- layer_out: bfloat16 [32768, 2048], P(('req', 'tok'))
The draws below stay inside these ranges and needn't reach their ends.
Inputs may be any that keep to these rules, and one draw needn't show every extreme that they name: Each row holds one owner's 4 prompt lengths in order; they sum to 1024, and the longest is 511 in every row.
All inputs are finite; a program needn't handle non-finite values.
Results may differ from the reference program's by a relative error of at most 0.02.
Values may be sent and summed in bfloat16 or wider, within the bound.
A program may use at most 128 MiB of HBM per device.

```python
import math
import jax
import jax.numpy as jnp
import numpy as np
from jax import lax

H = 32
HD = 64
MODEL_WIDTH = 2048
ROT = 16
HIDDEN_HALF = 2816
ADAPTER_RANK = 16
ADAPTER_TOTAL = 64
LMAX = 511
S_OWN = 1024
OWNER_REQUESTS = 4
OWNERS = 32
TOKENS = 32768
N_TOK = 4


def draw_tokens(key, part):
    subkeys = jax.random.split(key, 3)
    row_scale = jnp.exp(jax.random.uniform(subkeys[0], (TOKENS, 1), jnp.float32, math.log(0.1), math.log(1.0)))
    col_scale = jnp.exp(jax.random.uniform(subkeys[1], (1, MODEL_WIDTH), jnp.float32, math.log(0.3), math.log(3.0)))
    values = row_scale * col_scale * jnp.clip(jax.random.normal(subkeys[2], (TOKENS, MODEL_WIDTH), jnp.float32), -4.0, 4.0)
    return values.astype(jnp.bfloat16)


def with_ends(result, stream_key, low, high):
    longest = result.shape.index(max(result.shape))
    spots = []
    for shift in (0, 1):
        where = [jax.random.randint(jax.random.fold_in(stream_key, axis), (), 0, length) for axis, length in enumerate(result.shape)]
        where[longest] = (where[longest] + shift) % result.shape[longest]
        spots.append(tuple(where))
    return result.at[spots[0]].set(low).at[spots[1]].set(high)


def levels(rng, shape, cuts, low, high):
    loudness, own = 1.0, jax.random.fold_in(rng, 6)
    for position, parts in cuts:
        heights = jnp.exp(jax.random.uniform(jax.random.fold_in(own, position), (parts,), jnp.float32, low / len(cuts), high / len(cuts)))
        loudness = loudness * jnp.repeat(heights, shape[position] // parts).reshape([-1 if axis == position else 1 for axis in range(len(shape))])
    return loudness


def split_up(number_of, total, reach, lean):
    weights = [(1 << 20) // math.isqrt(standing ** lean) + 1 for standing in range(2, number_of + 1)]
    surplus, counts = total - reach - (number_of - 1), [1] * (number_of - 1)
    while surplus > 0:
        candidates = [i for i in range(number_of - 1) if counts[i] < reach]
        whole, left = sum([weights[i] for i in candidates]), surplus
        for i in candidates:
            extra = min(reach - counts[i], max(1, left * weights[i] // whole), surplus)
            counts[i] = counts[i] + extra
            surplus = surplus - extra
    return np.array([reach] + counts)


def uneven_parts(stream_key, number_of, total, limit, slope):
    if number_of == 2:
        one = jax.random.randint(stream_key, (), max(1, total - limit), min(limit, total - 1) + 1)
        return jnp.stack([one, total - one])
    sizes = jnp.asarray(split_up(number_of, total, limit, slope), jnp.int32)
    pairs = (number_of - 1) // 2
    source_of, receiver = sizes[1:1 + 2 * pairs:2], sizes[2:2 + 2 * pairs:2]
    margin = jnp.minimum(source_of - 1, limit - receiver)
    passed = jax.random.randint(jax.random.fold_in(stream_key, 1), (pairs,), 0, 1 << 20) % (margin + 1)
    sizes = sizes.at[1:1 + 2 * pairs:2].set(source_of - passed).at[2:2 + 2 * pairs:2].set(receiver + passed)
    return sizes[jax.random.permutation(jax.random.fold_in(stream_key, 2), number_of)]


def bell_draw(own_key, extent, width, bound, cuts=(), kind=jnp.bfloat16):
    factor_of = levels(own_key, extent, cuts, -0.22, 0.18) if cuts else 1.0
    values = jax.random.normal(own_key, extent, jnp.float32) * width * factor_of
    return jnp.minimum(jnp.maximum(values, -bound), bound).astype(kind)


def setup_inputs(seed: int = 0) -> dict:
    key_of = jax.random.split(jax.random.key(seed), 21)
    tokens = draw_tokens(jax.random.fold_in(key_of[20], 71), 0)
    attention_norm_gain = jnp.clip(1.0 + 0.18 * jax.random.normal(key_of[1], (MODEL_WIDTH,), jnp.float32), 0.1, 1.9)
    attention_norm_bias = bell_draw(key_of[2], (MODEL_WIDTH,), 0.3, 1.75, (), jnp.float32)
    query_key_value_matrix = bell_draw(key_of[3], (3, MODEL_WIDTH, MODEL_WIDTH), MODEL_WIDTH ** -0.5, 0.125, ((1, 32), (2, 4)))
    query_key_value_bias = bell_draw(key_of[4], (3, MODEL_WIDTH), 0.5, 3.0, ((1, 4),), jnp.float32)
    output_matrix = bell_draw(key_of[5], (N_TOK, MODEL_WIDTH // N_TOK, MODEL_WIDTH), MODEL_WIDTH ** -0.5, 0.125, ((0, 4), (1, 32)))
    feedforward_norm_gain = jnp.clip(1.0 + 0.18 * jax.random.normal(key_of[6], (MODEL_WIDTH,), jnp.float32), 0.1, 1.9)
    feedforward_norm_bias = bell_draw(key_of[7], (MODEL_WIDTH,), 0.3, 1.75, (), jnp.float32)
    gate_up_matrix = bell_draw(key_of[8], (2, MODEL_WIDTH, HIDDEN_HALF), MODEL_WIDTH ** -0.5, 0.125, ((1, 32), (2, 4)))
    down_matrix = bell_draw(key_of[9], (N_TOK, HIDDEN_HALF // N_TOK, MODEL_WIDTH), HIDDEN_HALF ** -0.5, 0.109375, ((0, 4), (1, 32)))
    adapter_input_query_key_value = bell_draw(key_of[10], (ADAPTER_TOTAL, 3 * ADAPTER_RANK, MODEL_WIDTH), MODEL_WIDTH ** -0.5, 0.125, ((2, 32),))
    adapter_output_query_key_value = bell_draw(key_of[11], (ADAPTER_TOTAL, 3 * ADAPTER_RANK, N_TOK, MODEL_WIDTH // N_TOK), (4 * ADAPTER_RANK) ** -0.5, 0.75, ((2, 4), (3, 32)))
    adapter_input_output = bell_draw(key_of[12], (ADAPTER_TOTAL, ADAPTER_RANK, N_TOK, MODEL_WIDTH // N_TOK), MODEL_WIDTH ** -0.5, 0.125, ((2, 4), (3, 32)))
    adapter_output_projection = bell_draw(key_of[13], (ADAPTER_TOTAL, ADAPTER_RANK, MODEL_WIDTH), (4 * ADAPTER_RANK) ** -0.5, 0.75, ((2, 32),))
    adapter_input_gate_up = bell_draw(key_of[14], (ADAPTER_TOTAL, 2 * ADAPTER_RANK, MODEL_WIDTH), MODEL_WIDTH ** -0.5, 0.125, ((2, 32),))
    adapter_output_gate_up = bell_draw(key_of[15], (ADAPTER_TOTAL, 2 * ADAPTER_RANK, N_TOK, HIDDEN_HALF // N_TOK), (4 * ADAPTER_RANK) ** -0.5, 0.75, ((2, 4), (3, 32)))
    adapter_input_down = bell_draw(key_of[16], (ADAPTER_TOTAL, ADAPTER_RANK, N_TOK, HIDDEN_HALF // N_TOK), HIDDEN_HALF ** -0.5, 0.109375, ((2, 4), (3, 32)))
    adapter_output_down = bell_draw(key_of[17], (ADAPTER_TOTAL, ADAPTER_RANK, MODEL_WIDTH), (4 * ADAPTER_RANK) ** -0.5, 0.75, ((2, 32),))
    lengths = jax.vmap(lambda own: uneven_parts(own, OWNER_REQUESTS, S_OWN, LMAX, 1))(jax.random.split(key_of[18], OWNERS)).reshape((OWNERS, OWNER_REQUESTS)).astype(jnp.int32)
    adapter_per_request = with_ends(jax.random.randint(key_of[19], (OWNERS, OWNER_REQUESTS), 0, ADAPTER_TOTAL), jax.random.fold_in(key_of[19], 1), 0, ADAPTER_TOTAL - 1).astype(jnp.int32)
    return dict(tokens=tokens, attention_norm_gain=attention_norm_gain, attention_norm_bias=attention_norm_bias, query_key_value_matrix=query_key_value_matrix, query_key_value_bias=query_key_value_bias, output_matrix=output_matrix, feedforward_norm_gain=feedforward_norm_gain, feedforward_norm_bias=feedforward_norm_bias, gate_up_matrix=gate_up_matrix, down_matrix=down_matrix, adapter_input_query_key_value=adapter_input_query_key_value, adapter_output_query_key_value=adapter_output_query_key_value, adapter_input_output=adapter_input_output, adapter_output_projection=adapter_output_projection, adapter_input_gate_up=adapter_input_gate_up, adapter_output_gate_up=adapter_output_gate_up, adapter_input_down=adapter_input_down, adapter_output_down=adapter_output_down, lengths=lengths, adapter_per_request=adapter_per_request)


def layer_norm(values, gain_vec, shift_bias):
    row_mean = lax.optimization_barrier(jnp.mean(values, axis=-1, keepdims=True))
    centered = values - row_mean
    variance = lax.optimization_barrier(jnp.mean(centered * centered, axis=-1, keepdims=True))
    return centered * lax.rsqrt(variance + 1e-05) * gain_vec + shift_bias

def rotate(values, positions):
    half_rot = ROT // 2
    frequency = jnp.exp(-math.log(10000.0) * (2.0 * jnp.arange(half_rot, dtype=jnp.float32) / ROT))
    angles = positions.astype(jnp.float32)[:, None] * frequency[None, :]
    cosine = jnp.cos(angles)[:, None, :]
    sine_part = jnp.sin(angles)[:, None, :]
    lower_half = values[..., :half_rot]
    upper_half = values[..., half_rot:ROT]
    return jnp.concatenate([lower_half * cosine - upper_half * sine_part, upper_half * cosine + lower_half * sine_part, values[..., ROT:]], axis=-1)

def request_layout(owner_lengths, row_count):
    request_end = jnp.cumsum(owner_lengths).astype(jnp.int32)
    request_begin = (request_end - owner_lengths).astype(jnp.int32)
    places = jnp.arange(row_count, dtype=jnp.int32)
    request_slot = lax.optimization_barrier(jnp.sum((places[:, None] >= request_end[None, :]).astype(jnp.int32), axis=1)).astype(jnp.int32)
    member_mask = request_slot[:, None] == jnp.arange(owner_lengths.shape[0], dtype=jnp.int32)[None, :]
    request_start = lax.optimization_barrier(jnp.sum(jnp.where(member_mask, request_begin[None, :], 0), axis=1)).astype(jnp.int32)
    return (places, request_slot, member_mask, request_start)

def rounded(values):
    return lax.optimization_barrier(values.astype(jnp.bfloat16)).astype(jnp.float32)

def pick_rank(operand, shrink, member_weight):
    all_ranks = jnp.einsum('tn,jkn->tjk', operand.astype(jnp.float32), shrink.astype(jnp.float32))
    chosen = rounded(lax.optimization_barrier(jnp.sum(member_weight[:, :, None] * all_ranks, axis=1)))
    return member_weight[:, :, None] * chosen[:, None, :]

def reference(tokens, attention_norm_gain, attention_norm_bias, query_key_value_matrix, query_key_value_bias, output_matrix, feedforward_norm_gain, feedforward_norm_bias, gate_up_matrix, down_matrix, adapter_input_query_key_value, adapter_output_query_key_value, adapter_input_output, adapter_output_projection, adapter_input_gate_up, adapter_output_gate_up, adapter_input_down, adapter_output_down, lengths, adapter_per_request):
    qkv_flat = jnp.transpose(query_key_value_matrix, (1, 0, 2)).reshape(MODEL_WIDTH, 3 * MODEL_WIDTH).astype(jnp.float32)
    gate_flat = jnp.transpose(gate_up_matrix, (1, 0, 2)).reshape(MODEL_WIDTH, 2 * HIDDEN_HALF).astype(jnp.float32)
    out_full = output_matrix.astype(jnp.float32)
    down_full = down_matrix.astype(jnp.float32)
    head_width = MODEL_WIDTH // N_TOK
    unit_width = HIDDEN_HALF // N_TOK
    score_scale = HD ** (-0.5)

    def owner_layer(owner_idx):
        owner_rows = lax.dynamic_slice_in_dim(tokens, owner_idx * S_OWN, S_OWN, 0).astype(jnp.float32)
        owner_lengths = lax.dynamic_index_in_dim(lengths, owner_idx, 0, keepdims=False)
        adapters_of_owner = lax.dynamic_index_in_dim(adapter_per_request, owner_idx, 0, keepdims=False)
        places, request_slot, member_mask, request_start = request_layout(owner_lengths, S_OWN)
        member_weight = member_mask.astype(jnp.float32)
        positions = places - request_start
        narrow_query_key_value = adapter_input_query_key_value[adapters_of_owner]
        widen_query_key_value = adapter_output_query_key_value[adapters_of_owner].reshape(OWNER_REQUESTS, 3, ADAPTER_RANK, MODEL_WIDTH).astype(jnp.float32)
        narrow_output = adapter_input_output[adapters_of_owner].reshape(OWNER_REQUESTS, ADAPTER_RANK, MODEL_WIDTH)
        widen_output = adapter_output_projection[adapters_of_owner].astype(jnp.float32)
        narrow_gate = adapter_input_gate_up[adapters_of_owner]
        widen_gate = adapter_output_gate_up[adapters_of_owner].reshape(OWNER_REQUESTS, 2, ADAPTER_RANK, HIDDEN_HALF).astype(jnp.float32)
        narrow_down = adapter_input_down[adapters_of_owner].reshape(OWNER_REQUESTS, ADAPTER_RANK, HIDDEN_HALF)
        widen_down = adapter_output_down[adapters_of_owner].astype(jnp.float32)
        normed = layer_norm(owner_rows, attention_norm_gain, attention_norm_bias).astype(jnp.bfloat16)
        low_qkv = pick_rank(normed, narrow_query_key_value, member_weight).reshape(S_OWN, OWNER_REQUESTS, 3, ADAPTER_RANK)
        mixed = jnp.dot(normed.astype(jnp.float32), qkv_flat).reshape(S_OWN, 3, MODEL_WIDTH) + query_key_value_bias[None]
        mixed = mixed + jnp.einsum('tjkr,jkrc->tkc', low_qkv, widen_query_key_value)
        query = rotate(mixed[:, 0].reshape(S_OWN, H, HD), positions).astype(jnp.bfloat16)
        key_rows = rotate(mixed[:, 1].reshape(S_OWN, H, HD), positions).astype(jnp.bfloat16)
        value_rows = mixed[:, 2].reshape(S_OWN, H, HD).astype(jnp.bfloat16)
        visible = (request_slot[:, None] == request_slot[None, :]) & (places[None, :] <= places[:, None])

        def head_attention(head_args):
            query_head, key_head, value_head = head_args
            scores = jnp.dot(query_head, key_head.T, preferred_element_type=jnp.float32) * score_scale
            weights = jnp.where(visible, jnp.exp(scores), 0.0)
            summed = jnp.dot(weights.astype(jnp.bfloat16), value_head, preferred_element_type=jnp.float32)
            return (summed / lax.optimization_barrier(jnp.sum(weights, axis=1, keepdims=True))).astype(jnp.bfloat16)
        per_head = lax.map(head_attention, (jnp.transpose(query, (1, 0, 2)), jnp.transpose(key_rows, (1, 0, 2)), jnp.transpose(value_rows, (1, 0, 2))))
        attended = jnp.transpose(per_head, (1, 0, 2)).reshape(S_OWN, MODEL_WIDTH)
        out_sum = jnp.zeros((S_OWN, MODEL_WIDTH), jnp.float32)
        for block_idx in range(N_TOK):
            col_start = block_idx * head_width
            block_in = attended[:, col_start:col_start + head_width]
            low_out = pick_rank(block_in, narrow_output[:, :, col_start:col_start + head_width], member_weight)
            block_term = jnp.dot(block_in.astype(jnp.float32), out_full[block_idx]) + jnp.einsum('tjr,jrd->td', low_out, widen_output)
            out_sum = out_sum + rounded(block_term)
        residual = (owner_rows + out_sum).astype(jnp.bfloat16)
        normed2 = layer_norm(residual.astype(jnp.float32), feedforward_norm_gain, feedforward_norm_bias).astype(jnp.bfloat16)
        low_gate = pick_rank(normed2, narrow_gate, member_weight).reshape(S_OWN, OWNER_REQUESTS, 2, ADAPTER_RANK)
        gate_up = jnp.dot(normed2.astype(jnp.float32), gate_flat).reshape(S_OWN, 2, HIDDEN_HALF)
        gate_up = gate_up + jnp.einsum('tjkr,jkrf->tkf', low_gate, widen_gate)
        hidden = (jax.nn.silu(gate_up[:, 0]) * gate_up[:, 1]).astype(jnp.bfloat16)
        down_sum = jnp.zeros((S_OWN, MODEL_WIDTH), jnp.float32)
        for block_idx in range(N_TOK):
            col_start = block_idx * unit_width
            block_in = hidden[:, col_start:col_start + unit_width]
            low_down = pick_rank(block_in, narrow_down[:, :, col_start:col_start + unit_width], member_weight)
            block_term = jnp.dot(block_in.astype(jnp.float32), down_full[block_idx]) + jnp.einsum('tjr,jrd->td', low_down, widen_down)
            down_sum = down_sum + rounded(block_term)
        return (residual.astype(jnp.float32) + down_sum).astype(jnp.bfloat16)
    layers = lax.map(owner_layer, jnp.arange(OWNERS, dtype=jnp.int32))
    return layers.reshape(TOKENS, MODEL_WIDTH)
```

```python
import functools
import math

import jax
import jax.numpy as jnp
from jax import lax
from jax.experimental import pallas as pl
from jax.experimental.pallas import tpu as pltpu
from jax.sharding import PartitionSpec as P

HD = 64
ROT = 16
MESH = pl.DeviceIdType.MESH
VMEM = pl.BlockSpec(memory_space=pltpu.VMEM)
ANY = pl.BlockSpec(memory_space=pl.ANY)
SMEM = pl.BlockSpec(memory_space=pltpu.SMEM)
F32 = jnp.float32
BF16 = jnp.bfloat16


def layer_norm(values, gain_vec, shift_bias):
    row_mean = jnp.mean(values, axis=-1, keepdims=True)
    centered = values - row_mean
    variance = jnp.mean(centered * centered, axis=-1, keepdims=True)
    return centered * lax.rsqrt(variance + 1e-05) * gain_vec + shift_bias


def dot(left, right):
    return lax.dot_general(left, right, (((1,), (0,)), ((), ())), preferred_element_type=F32)


def dot_t(left, right):
    return lax.dot_general(left, right, (((1,), (1,)), ((), ())), preferred_element_type=F32)


def pick_kernel(ids, aq, wd, ag, wo, bq, bo, cg, cd, a_out, b_out, c_out):
    def eye(n):
        return (
            lax.broadcasted_iota(jnp.int32, (n, n), 0)
            == lax.broadcasted_iota(jnp.int32, (n, n), 1)
        ).astype(BF16)

    eye_a, eye_b, eye_c = eye(aq.shape[2]), eye(bq.shape[2]), eye(cg.shape[2])
    slots = 4

    def owner(g, carry):
        def rows(ref):
            return [ref[ids[g * slots + j]] for j in range(slots)]

        stack_a = jnp.concatenate(rows(aq) + rows(wd) + rows(ag) + rows(wo), axis=0)
        stack_b = jnp.concatenate(rows(bq) + rows(bo), axis=0)
        stack_c = jnp.concatenate(rows(cg) + rows(cd), axis=0)
        a_out[g] = dot_t(eye_a, stack_a).astype(BF16)
        b_out[g] = dot_t(eye_b, stack_b).astype(BF16)
        c_out[g] = dot_t(eye_c, stack_c).astype(BF16)
        return carry

    lax.fori_loop(0, a_out.shape[0], owner, 0)


def pick_adapters(ids, aq, wd, ag, wo, bq, bo, cg, cd):
    owners = ids.shape[0] // 4
    cols_a = 4 * (aq.shape[1] + wd.shape[1] + ag.shape[1] + wo.shape[1])
    cols_b = 4 * (bq.shape[1] + bo.shape[1])
    cols_c = 4 * (cg.shape[1] + cd.shape[1])
    return pl.pallas_call(
        pick_kernel,
        out_shape=[
            jax.ShapeDtypeStruct((owners, aq.shape[2], cols_a), BF16),
            jax.ShapeDtypeStruct((owners, bq.shape[2], cols_b), BF16),
            jax.ShapeDtypeStruct((owners, cg.shape[2], cols_c), BF16),
        ],
        in_specs=[SMEM] + [VMEM] * 8,
        out_specs=[VMEM] * 3,
        name="pick",
    )(ids, aq, wd, ag, wo, bq, bo, cg, cd)


def ring():
    n = lax.axis_size("tok")
    me = lax.axis_index("tok")
    return me, lax.rem(me + 1, n), lax.rem(me + n - 1, n), lax.rem(me + 2, n)


def greet(right, left):
    barrier = pltpu.get_barrier_semaphore()
    for neighbour in (left, right):
        pl.semaphore_signal(barrier, inc=1, device_id={"tok": neighbour}, device_id_type=MESH)
    pl.semaphore_wait(barrier, 2)


def send_to(source, target, send_sem, recv_sem, device):
    return pltpu.make_async_remote_copy(
        src_ref=source,
        dst_ref=target,
        send_sem=send_sem,
        recv_sem=recv_sem,
        device_id={"tok": device},
        device_id_type=MESH,
    )


def rows_of(block, rows, offset=0, size=None):
    return pl.ds(pl.multiple_of(block * rows + offset, rows // 2), rows if size is None else size)


class RingGather:
    def __init__(self, own, held, send, recv):
        me, right, left, opposite = ring()
        rows = own.shape[0]
        half = rows // 2
        low, high = pl.ds(0, half), pl.ds(half, half)
        mine_low = held.at[rows_of(me, rows, 0, half)]
        mine_high = held.at[rows_of(me, rows, half, half)]
        left_low = held.at[rows_of(left, rows, 0, half)]
        right_high = held.at[rows_of(right, rows, half, half)]
        self.first = [
            send_to(own.at[low], mine_low, send.at[0], recv.at[0], right),
            send_to(own.at[high], mine_high, send.at[1], recv.at[1], left),
            send_to(own.at[high], mine_high, send.at[2], recv.at[2], right),
            send_to(own.at[low], mine_low, send.at[3], recv.at[3], left),
        ]
        self.second = [
            send_to(left_low, left_low, send.at[4], recv.at[4], right),
            send_to(right_high, right_high, send.at[5], recv.at[5], left),
        ]

    def start(self):
        for copy in self.first:
            copy.start()

    def forward(self):
        for copy, onward in zip(self.first[:2], self.second):
            copy.wait_recv()
            onward.start()

    def neighbours(self):
        for copy in self.first[2:]:
            copy.wait_recv()

    def opposite(self):
        for copy in self.second:
            copy.wait_recv()

    def drain(self):
        for copy in self.first + self.second:
            copy.wait_send()


def gather_kernel(own, held, send, recv):
    me, right, left, _ = ring()
    greet(right, left)
    moves = RingGather(own, held, send, recv)
    moves.start()
    held[rows_of(me, own.shape[0]), :] = own[...]
    moves.forward()
    moves.neighbours()
    moves.opposite()
    moves.drain()


def gather_rows(own, count):
    rows, width = own.shape
    return pl.pallas_call(
        gather_kernel,
        out_shape=jax.ShapeDtypeStruct((rows * count, width), own.dtype),
        in_specs=[VMEM],
        out_specs=VMEM,
        scratch_shapes=[pltpu.SemaphoreType.DMA((6,)), pltpu.SemaphoreType.DMA((6,))],
        compiler_params=pltpu.CompilerParams(collective_id=0, has_side_effects=True),
        name="gather_rows",
    )(own)


def scatter_sum(term, total, far, to_right, to_left, mid_low, mid_high, from_left, from_right, send, recv):
    me, right, left, opposite = ring()
    rows = far.shape[0]
    half = rows // 2
    low, high = pl.ds(0, half), pl.ds(half, half)
    copies = [
        send_to(far.at[low], mid_low, send.at[0], recv.at[0], right),
        send_to(far.at[high], mid_high, send.at[1], recv.at[1], left),
        send_to(to_right.at[high], from_left.at[high], send.at[2], recv.at[2], right),
        send_to(to_left.at[low], from_right.at[low], send.at[3], recv.at[3], left),
        send_to(to_right.at[low], from_left.at[low], send.at[4], recv.at[4], right),
        send_to(to_left.at[high], from_right.at[high], send.at[5], recv.at[5], left),
    ]
    term(opposite, far)
    copies[0].start()
    copies[1].start()
    term(right, to_right)
    copies[2].start()
    term(left, to_left)
    copies[3].start()
    copies[0].wait_recv()
    to_right[low, :] = (to_right[low, :].astype(F32) + mid_low[...].astype(F32)).astype(BF16)
    copies[4].start()
    copies[1].wait_recv()
    to_left[high, :] = (to_left[high, :].astype(F32) + mid_high[...].astype(F32)).astype(BF16)
    copies[5].start()
    term(me, total)
    for copy in copies[2:]:
        copy.wait_recv()
    for copy in copies:
        copy.wait_send()
    total[...] = total[...] + from_left[...].astype(F32) + from_right[...].astype(F32)


def sum_scratch(rows, width):
    half = rows // 2
    return [
        pltpu.VMEM((rows, width), F32),
        pltpu.VMEM((rows, width), BF16),
        pltpu.VMEM((rows, width), BF16),
        pltpu.VMEM((rows, width), BF16),
        pltpu.VMEM((half, width), BF16),
        pltpu.VMEM((half, width), BF16),
        pltpu.VMEM((rows, width), BF16),
        pltpu.VMEM((rows, width), BF16),
        pltpu.SemaphoreType.DMA((6,)),
        pltpu.SemaphoreType.DMA((6,)),
    ]


def of_slot(slot, columns, per_slot):
    owner = lax.broadcasted_iota(jnp.int32, (slot.shape[0], columns), 1) // per_slot
    return slot == owner


def attention_kernel(
    x_ref, w_ref, bias_ref, narrow_ref, widen_ref, cos_ref, up_ref, down_ref, slot_ref, keyslot_ref,
    out_ref, q_s, k_s, v_s, bias_s,
):
    step = pl.program_id(0)
    rows = x_ref.shape[0]
    width = out_ref.shape[1]
    pairs = width // 128
    x = x_ref[...]
    slot = slot_ref[pl.ds(pl.multiple_of(step * rows, rows), rows), :]
    columns = narrow_ref.shape[1]
    low = dot(x, narrow_ref[...])
    low = jnp.where(of_slot(slot, columns, columns // 4), low, 0.0)
    kind = (lax.broadcasted_iota(jnp.int32, low.shape, 1) // 16) % 3
    here = pl.ds(pl.multiple_of(step * rows, rows), rows)
    cosine, rise, fall = cos_ref[...], up_ref[...], down_ref[...]
    lane = lax.broadcasted_iota(jnp.int32, (rows, 128), 1)
    for i in range(3):
        part = dot(x, w_ref[:, i * width : (i + 1) * width]) + bias_ref[i : i + 1, :]
        part = part + dot_t(jnp.where(kind == i, low, 0.0).astype(BF16), widen_ref[...])
        for p in range(pairs):
            block = part[:, p * 128 : (p + 1) * 128]
            if i < 2:
                block = (
                    block * cosine
                    + pltpu.roll(block, 120, 1) * rise
                    + pltpu.roll(block, 8, 1) * fall
                )
            block = block.astype(BF16)
            if i == 0:
                zero = jnp.zeros_like(block)
                q_s[2 * p] = jnp.where(lane < 64, block, zero)
                q_s[2 * p + 1] = jnp.where(lane < 64, zero, block)
            elif i == 1:
                k_s[p, here, :] = block
            else:
                v_s[p, here, 0:128] = block
                v_s[p, here, 128:256] = jnp.ones_like(block)

    scale = HD ** (-0.5) * math.log2(math.e)

    def window(start, count):
        keys = pl.ds(pl.multiple_of(start * rows, rows), count * rows)
        span = (rows, count * rows)
        query_place = lax.broadcasted_iota(jnp.int32, span, 0) + step * rows
        key_place = lax.broadcasted_iota(jnp.int32, span, 1) + start * rows
        visible = (slot == keyslot_ref[:, keys]) & (key_place <= query_place)
        bias_s[:, : count * rows] = jnp.where(visible, 0.0, -jnp.inf)

        def pair(p, carry):
            key = k_s[p, keys, :]
            value = v_s[p, keys, :]
            both = []
            for side in range(2):
                scores = dot_t(q_s[2 * p + side], key)
                weight = jnp.exp2(scores * scale + bias_s[:, : count * rows]).astype(BF16)
                both.append(dot(weight, value))
            even = both[0][:, :128] / both[0][:, 128:]
            odd = both[1][:, :128] / both[1][:, 128:]
            out_ref[:, pl.ds(pl.multiple_of(p * 128, 128), 128)] = jnp.where(
                lane < 64, even, odd
            ).astype(BF16)
            return carry

        lax.fori_loop(0, pairs, pair, 0)

    @pl.when(step == 0)
    def _():
        window(0, 1)

    @pl.when(step == 1)
    def _():
        window(0, 2)

    @pl.when(step >= 2)
    def _():
        window(step - 2, 3)


def attend(x, first, width, bias, narrow, widen, cosine, rise, fall, slot, keyslot):
    count, depth = x.shape
    rows = 256
    pairs = width // 128
    table = pl.BlockSpec((rows, 128), lambda i: (i, 0))
    whole = lambda a: pl.BlockSpec(a.shape, lambda i: (0, 0))
    return pl.pallas_call(
        attention_kernel,
        out_shape=jax.ShapeDtypeStruct((count, width), BF16),
        grid=(count // rows,),
        in_specs=[
            pl.BlockSpec((rows, depth), lambda i: (i, 0)),
            pl.BlockSpec((depth, 3 * width), lambda i: (0, 0)),
            whole(bias),
            whole(narrow),
            whole(widen),
            table,
            table,
            table,
            whole(slot),
            whole(keyslot),
        ],
        out_specs=pl.BlockSpec((rows, width), lambda i: (i, 0)),
        scratch_shapes=[
            pltpu.VMEM((2 * pairs, rows, 128), BF16),
            pltpu.VMEM((pairs, count, 128), BF16),
            pltpu.VMEM((pairs, count, 256), BF16),
            pltpu.VMEM((rows, 3 * rows), F32),
        ],
        compiler_params=pltpu.CompilerParams(dimension_semantics=("arbitrary",)),
        name="attend",
    )(x, first, bias, narrow, widen, cosine, rise, fall, slot, keyslot)


def output_kernel(
    att, first, narrow, widen, slot, tokens, gain, shift, residual, normed,
    weight, low_s, weight_sem, *scratch,
):
    me, right, left, _ = ring()
    shares = first.shape[0]
    width = first.shape[3]
    load = pltpu.make_async_copy(first.at[:, :, :, :], weight, weight_sem)
    load.start()
    greet(right, left)
    low = dot(att[...], narrow[...])
    columns = low.shape[1]
    low_s[...] = jnp.where(of_slot(slot[...], columns, columns // 4), low, 0.0).astype(BF16)
    load.wait()
    rows = tokens.shape[0]
    blocks = tokens.shape[1] // width

    def term(block, ref):
        here = rows_of(block, rows)

        def column(q, carry):
            at = pl.ds(pl.multiple_of(q * width, width), width)
            matrix = weight[:, q].reshape(att.shape[1], width)
            value = dot(att[here, :], matrix) + dot_t(low_s[here, :], widen[at, :])
            ref[:, at] = value.astype(ref.dtype)
            return carry

        lax.fori_loop(0, blocks, column, 0)

    total = scratch[0]
    scatter_sum(term, *scratch)
    for part in range(4):
        here = pl.ds(part * rows // 4, rows // 4)
        kept = (tokens[here, :].astype(F32) + total[here, :]).astype(BF16)
        residual[here, :] = kept
        normed[here, :] = layer_norm(kept.astype(F32), gain[...], shift[...]).astype(BF16)


def project(att, first, narrow, widen, slot, tokens, gain, shift):
    rows, width = tokens.shape
    shape = jax.ShapeDtypeStruct((rows, width), BF16)
    return pl.pallas_call(
        output_kernel,
        out_shape=[shape, shape],
        in_specs=[VMEM, ANY] + [VMEM] * 6,
        out_specs=[VMEM, VMEM],
        scratch_shapes=[
            pltpu.VMEM(first.shape, BF16),
            pltpu.VMEM((att.shape[0], narrow.shape[1]), BF16),
            pltpu.SemaphoreType.DMA,
        ]
        + sum_scratch(rows, width),
        compiler_params=pltpu.CompilerParams(collective_id=1, has_side_effects=True),
        name="project",
    )(att, first, narrow, widen, slot, tokens, gain, shift)


def feed_kernel(
    own, residual, second, down, narrow_gate, widen_gate, narrow_down, widen_down, slot, out,
    weight, held, hidden, low_s, weight_sem, gather_send, gather_recv, *scratch,
):
    me, right, left, opposite = ring()
    load = pltpu.make_async_copy(second.at[:, pl.ds(0, weight.shape[1])], weight, weight_sem)
    load.start()
    greet(right, left)
    moves = RingGather(own, held, gather_send, gather_recv)
    moves.start()
    rows, width = own.shape
    units = hidden.shape[1]
    held[rows_of(me, rows), :] = own[...]
    load.wait()

    def widen(block):
        here = rows_of(block, rows)
        x = held[here, :]
        low = dot(x, narrow_gate[...])
        columns = low.shape[1]
        low = jnp.where(of_slot(slot[here, :], columns, columns // 4), low, 0.0)
        kind = (lax.broadcasted_iota(jnp.int32, low.shape, 1) // 16) % 2
        both = dot(x, weight[...])
        gate = both[:, :units] + dot_t(jnp.where(kind == 0, low, 0.0).astype(BF16), widen_gate[...])
        up = both[:, units:] + dot_t(jnp.where(kind == 1, low, 0.0).astype(BF16), widen_gate[...])
        value = (gate / (1.0 + jnp.exp(-gate)) * up).astype(BF16)
        hidden[here, :] = value
        low_down = dot(value, narrow_down[...])
        columns = low_down.shape[1]
        low_s[here, :] = jnp.where(
            of_slot(slot[here, :], columns, columns // 4), low_down, 0.0
        ).astype(BF16)

    widen(me)
    moves.forward()
    moves.neighbours()

    def near(i, carry):
        widen(lax.rem(me + 1 + 2 * i, 4))
        return carry

    lax.fori_loop(0, 2, near, 0)
    moves.opposite()
    widen(opposite)
    moves.drain()
    step = 512

    def term(block, ref):
        here = rows_of(block, rows)

        def column(q, carry):
            at = pl.ds(pl.multiple_of(q * step, step), step)
            value = dot(hidden[here, :], down[:, at]) + dot_t(low_s[here, :], widen_down[at, :])
            ref[:, at] = value.astype(ref.dtype)
            return carry

        lax.fori_loop(0, width // step, column, 0)

    scatter_sum(term, *scratch)
    out[...] = (residual[...].astype(F32) + scratch[0][...]).astype(BF16)


def feed(own, residual, second, down, narrow_gate, widen_gate, narrow_down, widen_down, slot):
    rows, width = own.shape
    count = slot.shape[0]
    units = down.shape[0]
    return pl.pallas_call(
        feed_kernel,
        out_shape=jax.ShapeDtypeStruct((rows, width), BF16),
        in_specs=[VMEM, VMEM, ANY] + [VMEM] * 6,
        out_specs=VMEM,
        scratch_shapes=[
            pltpu.VMEM((second.shape[0], 2 * units), BF16),
            pltpu.VMEM((count, width), BF16),
            pltpu.VMEM((count, units), BF16),
            pltpu.VMEM((count, narrow_down.shape[1]), BF16),
            pltpu.SemaphoreType.DMA,
            pltpu.SemaphoreType.DMA((6,)),
            pltpu.SemaphoreType.DMA((6,)),
        ]
        + sum_scratch(rows, width),
        compiler_params=pltpu.CompilerParams(collective_id=2, has_side_effects=True),
        name="feed",
    )(own, residual, second, down, narrow_gate, widen_gate, narrow_down, widen_down, slot)


def rotation_tables(positions):
    half = ROT // 2
    frequency = jnp.exp(-math.log(10000.0) * (2.0 * jnp.arange(half, dtype=F32) / ROT))
    angles = positions.astype(F32)[:, None] * frequency[None, :]
    cosine, sine = jnp.cos(angles), jnp.sin(angles)
    count = positions.shape[0]
    zero = jnp.zeros((count, half), F32)
    rest = jnp.zeros((count, HD - ROT), F32)
    cos_head = jnp.concatenate([cosine, cosine, rest + 1.0], axis=1)
    rise_head = jnp.concatenate([-sine, zero, rest], axis=1)
    fall_head = jnp.concatenate([zero, sine, rest], axis=1)
    return [jnp.concatenate([t, t], axis=1) for t in (cos_head, rise_head, fall_head)]


def on_device(
    tokens,
    attention_norm_gain,
    attention_norm_bias,
    query_key_value_matrix,
    query_key_value_bias,
    output_matrix,
    feedforward_norm_gain,
    feedforward_norm_bias,
    gate_up_matrix,
    down_matrix,
    adapter_input_query_key_value,
    adapter_output_query_key_value,
    adapter_input_output,
    adapter_output_projection,
    adapter_input_gate_up,
    adapter_output_gate_up,
    adapter_input_down,
    adapter_output_down,
    lengths,
    adapter_per_request,
):
    tok_count = lax.axis_size("tok")
    owners = lax.axis_size("req")
    rows, width = tokens.shape
    count = rows * tok_count
    share = query_key_value_matrix.shape[1]
    head_cols = query_key_value_matrix.shape[2]
    units = gate_up_matrix.shape[2]
    fold = width // head_cols
    qkv = jnp.transpose(query_key_value_matrix, (1, 0, 2)).reshape(share, 3 * head_cols)
    out_rows = output_matrix.shape[1]
    out_fold = jnp.transpose(
        output_matrix[0].reshape(out_rows, fold, head_cols), (1, 0, 2)
    ).reshape(share, head_cols)
    first = lax.all_gather(
        jnp.concatenate([qkv, out_fold], axis=1), "req", axis=0, tiled=True
    )
    gate_up = jnp.transpose(gate_up_matrix, (1, 0, 2)).reshape(share, 2 * units)
    down_rows = down_matrix.shape[1]
    down_pad = jnp.pad(down_matrix[0], ((0, share // 2 - down_rows), (0, 0)))
    down_fold = jnp.concatenate([down_pad[:, : width // 2], down_pad[:, width // 2 :]], axis=0)
    second_part = jnp.concatenate([gate_up, down_fold], axis=1)
    second_part, first = lax.optimization_barrier((second_part, first))
    second = lax.all_gather(second_part, "req", axis=0, tiled=True)

    def flat(divided):
        return divided.reshape(divided.shape[0], divided.shape[1], divided.shape[3])

    ids = adapter_per_request.reshape(-1)
    pack_a, pack_b, pack_c = pick_adapters(
        ids,
        adapter_input_query_key_value,
        adapter_output_down,
        adapter_input_gate_up,
        adapter_output_projection,
        flat(adapter_output_query_key_value),
        flat(adapter_input_output),
        flat(adapter_output_gate_up),
        flat(adapter_input_down),
    )

    def trade(pack):
        return lax.all_to_all(pack, "req", split_axis=0, concat_axis=0, tiled=True).reshape(
            owners * pack.shape[1], pack.shape[2]
        )

    got_a, got_b, got_c = trade(pack_a), trade(pack_b), trade(pack_c)
    c_qkv = 4 * adapter_input_query_key_value.shape[1]
    c_one = 4 * adapter_output_down.shape[1]
    c_two = 4 * adapter_input_gate_up.shape[1]
    narrow_qkv = got_a[:, :c_qkv]
    widen_down = got_a[:, c_qkv : c_qkv + c_one]
    narrow_gate = got_a[:, c_qkv + c_one : c_qkv + c_one + c_two]
    widen_out = got_a[:, c_qkv + c_one + c_two :]
    widen_qkv, narrow_out = got_b[:, :c_qkv], got_b[:, c_qkv:]
    widen_gate, narrow_down = got_c[:, :c_two], got_c[:, c_two:]

    request_end = jnp.cumsum(lengths[0])
    request_begin = request_end - lengths[0]
    places = jnp.arange(count, dtype=jnp.int32)
    slot = jnp.sum((places[:, None] >= request_end[None, :]).astype(jnp.int32), axis=1)
    member = slot[:, None] == jnp.arange(lengths.shape[1], dtype=jnp.int32)[None, :]
    begin = jnp.sum(jnp.where(member, request_begin[None, :], 0), axis=1)
    cosine, rise, fall = rotation_tables(places - begin)
    slot_column, slot_row = slot[:, None], slot[None, :]

    normed = layer_norm(tokens.astype(F32), attention_norm_gain, attention_norm_bias).astype(BF16)
    gathered = gather_rows(normed, tok_count)
    attended = attend(
        gathered, first, head_cols, query_key_value_bias, narrow_qkv, widen_qkv,
        cosine, rise, fall, slot_column, slot_row,
    )
    out_shares = first[:, 3 * head_cols :].reshape(owners, fold, out_rows, head_cols)
    residual, normed2 = project(
        attended, out_shares, narrow_out, widen_out, slot_column, tokens,
        feedforward_norm_gain[None], feedforward_norm_bias[None],
    )
    down = (
        second[:, 2 * units :]
        .reshape(owners, 2, share // 2, width // 2)[:, :, :down_rows, :]
        .transpose(0, 2, 1, 3)
        .reshape(owners * down_rows, width)
    )
    return feed(
        normed2, residual, second, down, narrow_gate, widen_gate, narrow_down, widen_down, slot_column
    )


def solution(mesh):
    in_specs = (
        P(("req", "tok"), None),
        P(),
        P(),
        P(None, "req", "tok"),
        P(None, "tok"),
        P("tok", "req", None),
        P(),
        P(),
        P(None, "req", "tok"),
        P("tok", "req", None),
        P(None, None, "req"),
        P(None, None, "tok", "req"),
        P(None, None, "tok", "req"),
        P(None, None, "req"),
        P(None, None, "req"),
        P(None, None, "tok", "req"),
        P(None, None, "tok", "req"),
        P(None, None, "req"),
        P("req", None),
        P(),
    )
    out_specs = P(("req", "tok"), None)
    return jax.shard_map(
        on_device, mesh=mesh, in_specs=in_specs, out_specs=out_specs, check_vma=False
    )
```
